32 devices in a mesh: dp: 8 (over z, y), ctx: 4 (over x, core).
Axes of the slice: x: 2, y: 2, z: 4, core: 2. Of those that a mesh axis runs over, the one named last changes fastest.
Arguments:
- hidden_in: float32 [4096, 1024], P(('dp', 'ctx')), may hold values from -6 to 6
- positions: int32 [4096], P(('dp', 'ctx')), may hold values from 0 to 511, as said below
- mixer_params: float32 [32, 197760], P(('dp', 'ctx'))
- feed_params: float32 [32, 196736], P(('dp', 'ctx'))
- mixer_first: float32 [32, 197760], P(('dp', 'ctx')), may hold values from -96 to 96
- feed_first: float32 [32, 196736], P(('dp', 'ctx')), may hold values from -96 to 96
- mixer_second: float32 [32, 197760], P(('dp', 'ctx')), may hold values from 256 to 16384
- feed_second: float32 [32, 196736], P(('dp', 'ctx')), may hold values from 256 to 16384
- out_grad: float32 [4096, 1024], P(('dp', 'ctx')), may hold values from -6 to 6
Outputs:
- block_out: float32 [4096, 1024], P(('dp', 'ctx'))
- grad_input: float32 [4096, 1024], P(('dp', 'ctx'))
- mixer_grad: float32 [32, 197760], P(('dp', 'ctx'))
- feed_grad: float32 [32, 196736], P(('dp', 'ctx'))
- mixer_new: float32 [32, 197760], P(('dp', 'ctx'))
- feed_new: float32 [32, 196736], P(('dp', 'ctx'))
- mixer_first_new: float32 [32, 197760], P(('dp', 'ctx'))
- feed_first_new: float32 [32, 196736], P(('dp', 'ctx'))
- mixer_second_new: float32 [32, 197760], P(('dp', 'ctx'))
- feed_second_new: float32 [32, 196736], P(('dp', 'ctx'))
The draws below stay inside these ranges and needn't reach their ends.
Inputs may be any that keep to these rules, and one draw needn't show every extreme that they name: `positions`: each entry is 0 where a sequence starts and one more than the entry before it otherwise; every block of 512 rows starts a sequence at its first row; sequences hold at most 512 tokens and lengths vary.
All inputs are finite; a program needn't handle non-finite values.
Results may differ from the reference program's by a relative error of at most 0.019.
The reference program's roundings to bfloat16 on the way count: a program that leaves them out, or rounds other values in their place, can miss the bound.
Values may be sent and summed in bfloat16 or wider, within the bound.
No kernel may reach another device: no remote copies, remote signals or barrier semaphores. Data moves between devices by JAX's collectives and lax.ppermute only.
A program may use at most 384 MiB of HBM per device.

```python
import math
from functools import partial
import jax
import jax.numpy as jnp
from jax import lax

D = 1024
FF = 2048
HEADS_SSM = 24
HEAD_SSM = 64
STATE = 128
KERNEL = 4
HEADS = 8
KV_HEADS = 2
HD = 64
TOK_DEV = 128
STEP = 10
DI = 1536
CONV_COLS = 1792
QUERY_CHANNELS = 512
KEY_CHANNELS = 128
IN_COLS = 3352
QKV_COLS = 768
SA = 197760
SB = 196736
PACK = 512
TOKENS = 4096
N_CTX = 4
DEVICES = 32


def draw_positions(key, part):
    pack_count = TOKENS // PACK
    longest = min(512, PACK)
    lengths = jax.random.randint(key, (pack_count, PACK), 1, longest + 1)
    lengths = lengths.at[0, 0].set(longest)
    begins = jnp.cumsum(lengths, axis=1) - lengths
    row_ids = jnp.broadcast_to(jnp.arange(pack_count, dtype=jnp.int32)[:, None], (pack_count, PACK))
    flags = jnp.zeros((pack_count, PACK), jnp.int32).at[row_ids, begins].set(1, mode='drop')
    steps_row = jnp.broadcast_to(jnp.arange(PACK, dtype=jnp.int32)[None, :], (pack_count, PACK))
    latest = lax.cummax(jnp.where(flags > 0, steps_row, 0), axis=1)
    return (steps_row - latest).reshape(-1).astype(jnp.int32)


def weight_block(key, layout, spread):
    return jax.random.normal(key, layout, jnp.float32) * spread


def spread_rows(pieces, width, filler_key):
    flat = jnp.concatenate([member.reshape(-1) for member in pieces])
    extra = DEVICES * width - flat.shape[0]
    filler = jax.random.normal(filler_key, (extra,), jnp.float32) * 0.01
    return jnp.concatenate([flat, filler]).reshape(DEVICES, width)


def draw_mixer_params(key, part):
    pieces = [weight_block(jax.random.fold_in(key, 1), (D, IN_COLS), D ** (-0.5)), weight_block(jax.random.fold_in(key, 2), (DI, D), DI ** (-0.5)), weight_block(jax.random.fold_in(key, 3), (D, QKV_COLS), D ** (-0.5)), weight_block(jax.random.fold_in(key, 4), (QUERY_CHANNELS, D), 3.0 * QUERY_CHANNELS ** (-0.5)), weight_block(jax.random.fold_in(key, 15), (KERNEL, CONV_COLS), 0.5), jax.random.uniform(jax.random.fold_in(key, 16), (CONV_COLS,), jnp.float32, -0.5, 0.5), jax.random.uniform(jax.random.fold_in(key, 5), (D,), jnp.float32, 0.6, 1.4), jax.random.uniform(jax.random.fold_in(key, 6), (HEADS_SSM,), jnp.float32, -2.0, 1.0), jax.random.uniform(jax.random.fold_in(key, 7), (HEADS_SSM,), jnp.float32, -6.2, -1.2), jax.random.uniform(jax.random.fold_in(key, 8), (HEADS_SSM,), jnp.float32, 0.5, 1.5)]
    return spread_rows(pieces, SA, jax.random.fold_in(key, 9))


def draw_feed_params(key, part):
    pieces = [weight_block(jax.random.fold_in(key, 11), (D, 2 * FF), D ** (-0.5)), weight_block(jax.random.fold_in(key, 12), (FF, D), FF ** (-0.5)), jax.random.uniform(jax.random.fold_in(key, 13), (D,), jnp.float32, 0.6, 1.4)]
    return spread_rows(pieces, SB, jax.random.fold_in(key, 14))


def shard_levels(key, dims, split, low, largest):
    def one(axis_at, blocks):
        heights = jax.random.uniform(jax.random.fold_in(jax.random.fold_in(key, 6), axis_at), (blocks,), jnp.float32, low / len(split), largest / len(split))
        return jnp.repeat(jnp.exp(heights), dims[axis_at] // blocks).reshape((-1,) + (1,) * (len(dims) - axis_at - 1))

    gain = one(*split[0])
    for cut in split[1:]:
        gain = gain * one(*cut)
    return gain


def scatter_about(key, extent, scale, most, cuts=(), kind=jnp.bfloat16):
    values = scale * jax.random.normal(key, extent, jnp.float32)
    if cuts:
        values = values * shard_levels(key, extent, cuts, -0.22, 0.18)
    return jnp.clip(values, -most, most).astype(kind)


def setup_inputs(seed: int = 0) -> dict:
    key_list = jax.random.split(jax.random.key(seed), 10)
    return {
        "hidden_in": scatter_about(key_list[0], (TOKENS, D), 1.0, 6.0, ((0, 32),), jnp.float32),
        "positions": draw_positions(jax.random.fold_in(key_list[9], 71), 0),
        "mixer_params": draw_mixer_params(jax.random.fold_in(key_list[9], 71), 0),
        "feed_params": draw_feed_params(jax.random.fold_in(key_list[9], 71), 0),
        "mixer_first": scatter_about(key_list[4], (DEVICES, SA), (TOKENS ** 0.5 / 4), 96.0, ((0, 32),), jnp.float32),
        "feed_first": scatter_about(key_list[5], (DEVICES, SB), (TOKENS ** 0.5 / 4), 96.0, ((0, 32),), jnp.float32),
        "mixer_second": jnp.clip(jnp.exp(math.log(16384.0) - 4.158883 * jax.random.uniform(key_list[6], (DEVICES, SA), jnp.float32) ** shard_levels(key_list[6], (DEVICES, SA), ((0, 32),), -0.2, 0.2)), 256.0, 16384.0),
        "feed_second": jnp.clip(jnp.exp(math.log(16384.0) - 4.158883 * jax.random.uniform(key_list[7], (DEVICES, SB), jnp.float32) ** shard_levels(key_list[7], (DEVICES, SB), ((0, 32),), -0.2, 0.2)), 256.0, 16384.0),
        "out_grad": scatter_about(key_list[8], (TOKENS, D), 1.0, 6.0, ((0, 32),), jnp.float32),
    }


eps_norm = 1e-05
rope_base = 100000000000.0
neg_large = -1e+30
beta_one = 0.9
beta_two = 0.95
learn_rate = 0.01
decay_weight = 0.1
adam_eps = 1e-08
highest = lax.Precision.HIGHEST

def rms_norm(values, gain_vec):
    return values * lax.rsqrt(lax.optimization_barrier(jnp.mean(values * values, axis=-1, keepdims=True)) + eps_norm) * gain_vec

def swiglu(gate_up):
    return jax.nn.silu(gate_up[:, :FF]) * gate_up[:, FF:]

def gate_product(ssm_out, ssm_gate):
    return ssm_out * jax.nn.silu(ssm_gate)

def causal_conv(positions, extended, conv_weight, conv_bias):
    row_count = positions.shape[0]
    summed = jnp.broadcast_to(conv_bias[None, :], (row_count, conv_bias.shape[0]))
    for tap_index in range(KERNEL):
        first_row = KERNEL - 1 - tap_index
        earlier = extended[first_row:first_row + row_count]
        usable = (positions >= tap_index).astype(jnp.float32)[:, None]
        summed = summed + usable * earlier * conv_weight[tap_index][None, :]
    return jax.nn.silu(summed)

def mixer_layouts():
    return [(D, IN_COLS), (DI, D), (D, QKV_COLS), (QUERY_CHANNELS, D), (KERNEL, CONV_COLS), (CONV_COLS,), (D,), (HEADS_SSM,), (HEADS_SSM,), (HEADS_SSM,)]

def feed_layouts():
    return [(D, 2 * FF), (FF, D), (D,)]

def unflatten(flat, layouts):
    result = []
    cursor = 0
    for layout in layouts:
        length = math.prod(layout)
        result.append(flat[cursor:cursor + length].reshape(layout))
        cursor = cursor + length
    return result

def pack_rows(pieces, devices, width):
    flat = jnp.concatenate([member.reshape(-1) for member in pieces])
    flat = jnp.pad(flat, (0, devices * width - flat.shape[0]))
    return flat.reshape(devices, width)

def rope_tables(positions):
    half_dim = HD // 2
    frequency = jnp.exp(-jnp.log(rope_base) * jnp.arange(half_dim, dtype=jnp.float32) * 2.0 / HD)
    angles = positions.astype(jnp.float32)[:, None] * frequency[None, :]
    return (jnp.cos(angles), jnp.sin(angles))

def apply_rotary(values, cosine_table, sine_table, reverse):
    row_count = values.shape[0]
    half_dim = HD // 2
    per_head = values.reshape(row_count, -1, HD)
    first_half = per_head[..., :half_dim]
    second_half = per_head[..., half_dim:]
    cos_wide = cosine_table[:, None, :]
    sin_wide = sine_table[:, None, :]
    if reverse:
        rotated = jnp.concatenate([first_half * cos_wide + second_half * sin_wide, second_half * cos_wide - first_half * sin_wide], axis=-1)
    else:
        rotated = jnp.concatenate([first_half * cos_wide - second_half * sin_wide, second_half * cos_wide + first_half * sin_wide], axis=-1)
    return rotated.reshape(row_count, -1)

def attention_mask(positions, offset, key_count):
    query_index = offset + jnp.arange(positions.shape[0], dtype=jnp.int32)
    key_index = jnp.arange(key_count, dtype=jnp.int32)
    return (key_index[None, :] <= query_index[:, None]) & (key_index[None, :] >= (query_index - positions)[:, None])

def attend(queries, key_tile_rows, value_tile_rows, allowed):
    row_count = queries.shape[0]
    group_size = HEADS // KV_HEADS
    query_head_rows = queries.astype(jnp.float32).reshape(row_count, KV_HEADS, group_size, HD)
    key_heads = key_tile_rows.astype(jnp.float32).reshape(-1, KV_HEADS, HD)
    value_heads = value_tile_rows.astype(jnp.float32).reshape(-1, KV_HEADS, HD)
    scores = jnp.einsum('rkgd,skd->kgrs', query_head_rows, key_heads) * HD ** (-0.5)
    unnormed = jnp.exp(jnp.where(allowed[None, None], scores, neg_large))
    row_sum = lax.optimization_barrier(jnp.sum(unnormed, axis=-1, keepdims=True))
    unnormed_b = unnormed.astype(jnp.bfloat16).astype(jnp.float32)
    mixed = jnp.einsum('kgrs,skd->kgrd', unnormed_b, value_heads) / row_sum
    attended = jnp.transpose(mixed, (2, 0, 1, 3)).reshape(row_count, QUERY_CHANNELS)
    log_total = jnp.log(row_sum[..., 0])
    return (attended, log_total)

def attend_back(queries, key_tile_rows, value_tile_rows, attended_b, grad_att_b, log_total, allowed):
    row_count = queries.shape[0]
    group_size = HEADS // KV_HEADS
    query_head_rows = queries.astype(jnp.float32).reshape(row_count, KV_HEADS, group_size, HD)
    key_heads = key_tile_rows.astype(jnp.float32).reshape(-1, KV_HEADS, HD)
    value_heads = value_tile_rows.astype(jnp.float32).reshape(-1, KV_HEADS, HD)
    scores = jnp.einsum('rkgd,skd->kgrs', query_head_rows, key_heads) * HD ** (-0.5)
    probs = jnp.exp(jnp.where(allowed[None, None], scores - log_total[..., None], neg_large))
    gradient_heads = grad_att_b.astype(jnp.float32).reshape(row_count, KV_HEADS, group_size, HD)
    out_heads = attended_b.astype(jnp.float32).reshape(row_count, KV_HEADS, group_size, HD)
    grad_probs = jnp.einsum('rkgd,skd->kgrs', gradient_heads, value_heads)
    row_dot = jnp.transpose(lax.optimization_barrier(jnp.sum(gradient_heads * out_heads, axis=-1)), (1, 2, 0))
    gradient_scores = (probs * (grad_probs - row_dot[..., None]) * HD ** (-0.5)).astype(jnp.bfloat16).astype(jnp.float32)
    grad_queries = jnp.einsum('kgrs,skd->rkgd', gradient_scores, key_heads).reshape(row_count, QUERY_CHANNELS)
    gradient_keys = jnp.einsum('hxbe,bhxo->eho', gradient_scores, query_head_rows).reshape(-1, KEY_CHANNELS)
    probabilities_batch = probs.astype(jnp.bfloat16).astype(jnp.float32)
    gradient_values = jnp.einsum('hxbe,bhxo->eho', probabilities_batch, gradient_heads).reshape(-1, KEY_CHANNELS)
    return (grad_queries, gradient_keys, gradient_values)

def span_decays(step_raw, bias_step, log_rate):
    step_size = jax.nn.softplus(step_raw + bias_step[None, :])
    cumulative = jnp.cumsum(-jnp.exp(log_rate)[None, :] * step_size, axis=0)
    return (step_size, cumulative)

def scaled_input(ssm_input, step_size):
    row_count = ssm_input.shape[0]
    return ssm_input.reshape(row_count, HEADS_SSM, HEAD_SSM) * step_size[:, :, None]

def span_summary(segment, ssm_input, state_write, step_raw, bias_step, log_rate):
    step_size, cumulative = span_decays(step_raw, bias_step, log_rate)
    weighted = scaled_input(ssm_input, step_size)
    same_end = (segment == segment[-1]).astype(jnp.float32)
    end_weight = same_end[:, None] * jnp.exp(cumulative[-1][None, :] - cumulative)
    local_state = jnp.einsum('sh,shp,sn->hpn', end_weight, weighted, state_write, precision=highest)
    total_decay = jnp.exp(cumulative[-1]) * (segment[-1] == 0).astype(jnp.float32)
    return (total_decay, local_state)

def span_apply(segment, ssm_input, state_write, state_read, step_raw, bias_step, log_rate, skip_gain, state_in):
    step_size, cumulative = span_decays(step_raw, bias_step, log_rate)
    weighted = scaled_input(ssm_input, step_size)
    row_count = ssm_input.shape[0]
    row_order = jnp.arange(row_count, dtype=jnp.int32)
    allowed = (row_order[None, :] <= row_order[:, None]) & (segment[None, :] == segment[:, None])
    log_gaps = cumulative[:, None, :] - cumulative[None, :, :]
    decay_pairs = jnp.exp(jnp.where(allowed[:, :, None], log_gaps, neg_large))
    read_write = jnp.dot(state_read, state_write.T, precision=highest)
    inner_part = jnp.einsum('tsh,shp->thp', read_write[:, :, None] * decay_pairs, weighted, precision=highest)
    carried = (segment == 0).astype(jnp.float32)[:, None] * jnp.exp(cumulative)
    from_state = jnp.einsum('tn,hpn->thp', state_read, state_in, precision=highest) * carried[:, :, None]
    skip_part = skip_gain[None, :, None] * ssm_input.reshape(row_count, HEADS_SSM, HEAD_SSM)
    return (inner_part + from_state + skip_part).reshape(row_count, DI)

def span_full(segment, ssm_input, state_write, state_read, step_raw, bias_step, log_rate, skip_gain, state_in):
    total_decay, local_state = span_summary(segment, ssm_input, state_write, step_raw, bias_step, log_rate)
    output = span_apply(segment, ssm_input, state_write, state_read, step_raw, bias_step, log_rate, skip_gain, state_in)
    return (output, total_decay[:, None, None] * state_in + local_state)

def ssm_pack(segments, ssm_input, state_write, state_read, step_raw, bias_step, log_rate, skip_gain):
    state = jnp.zeros((HEADS_SSM, HEAD_SSM, STATE), jnp.float32)
    outputs = []
    for member_index in range(N_CTX):
        lower = member_index * TOK_DEV
        upper = lower + TOK_DEV
        result_rows, state = span_full(segments[member_index], ssm_input[lower:upper], state_write[lower:upper], state_read[lower:upper], step_raw[lower:upper], bias_step, log_rate, skip_gain, state)
        outputs.append(result_rows)
    return jnp.concatenate(outputs, axis=0)

def pack_pass(hidden_pack, position_pack, grad_pack, mixer, feed):
    w_in, w_ssm_out, w_qkv, w_attn_out, conv_weight, conv_bias, gain_one, bias_step, log_rate, skip_gain = mixer
    w_gate_up, w_down, gain_two = feed
    bias_step = bias_step.astype(jnp.float32)
    log_rate = log_rate.astype(jnp.float32)
    skip_gain = skip_gain.astype(jnp.float32)
    normed_one, norm_one_back = jax.vjp(rms_norm, hidden_pack, gain_one.astype(jnp.float32))
    normed_b = normed_one.astype(jnp.bfloat16)
    projected = jnp.dot(normed_b, w_in, preferred_element_type=jnp.float32)
    ssm_gate = projected[:, :DI]
    conv_input = projected[:, DI:DI + CONV_COLS]
    step_raw = projected[:, DI + CONV_COLS:]
    extended = jnp.concatenate([jnp.zeros((KERNEL - 1, CONV_COLS), jnp.float32), conv_input], axis=0)
    conv_out, conv_back = jax.vjp(partial(causal_conv, position_pack), extended, conv_weight.astype(jnp.float32), conv_bias.astype(jnp.float32))
    ssm_input = conv_out[:, :DI]
    state_write = conv_out[:, DI:DI + STATE]
    state_read = conv_out[:, DI + STATE:]
    segments = []
    for member_index in range(N_CTX):
        starts = (position_pack[member_index * TOK_DEV:(member_index + 1) * TOK_DEV] == 0).astype(jnp.int32)
        segments.append(jnp.cumsum(starts))
    ssm_out, ssm_back = jax.vjp(partial(ssm_pack, segments), ssm_input, state_write, state_read, step_raw, bias_step, log_rate, skip_gain)
    gated, gate_back = jax.vjp(gate_product, ssm_out, ssm_gate)
    gated_b = gated.astype(jnp.bfloat16)
    mamba_branch = jnp.dot(gated_b, w_ssm_out, preferred_element_type=jnp.float32)
    query_key_value = jnp.dot(normed_b, w_qkv, preferred_element_type=jnp.float32)
    cosine_table, sine_table = rope_tables(position_pack)
    queries = apply_rotary(query_key_value[:, :QUERY_CHANNELS], cosine_table, sine_table, False).astype(jnp.bfloat16)
    key_tile_rows = apply_rotary(query_key_value[:, QUERY_CHANNELS:QUERY_CHANNELS + KEY_CHANNELS], cosine_table, sine_table, False).astype(jnp.bfloat16)
    value_tile_rows = query_key_value[:, QUERY_CHANNELS + KEY_CHANNELS:].astype(jnp.bfloat16)
    allowed = attention_mask(position_pack, 0, PACK)
    attended, log_total = attend(queries, key_tile_rows, value_tile_rows, allowed)
    attended_b = attended.astype(jnp.bfloat16)
    attn_branch = jnp.dot(attended_b, w_attn_out, preferred_element_type=jnp.float32)
    residual = hidden_pack + mamba_branch + attn_branch
    normed_two, norm_two_back = jax.vjp(rms_norm, residual, gain_two.astype(jnp.float32))
    normed_two_b = normed_two.astype(jnp.bfloat16)
    gate_up = jnp.dot(normed_two_b, w_gate_up, preferred_element_type=jnp.float32)
    activated, swiglu_back = jax.vjp(swiglu, gate_up)
    activated_b = activated.astype(jnp.bfloat16)
    block_out = residual + jnp.dot(activated_b, w_down, preferred_element_type=jnp.float32)
    grad_b = grad_pack.astype(jnp.bfloat16)
    grad_w_down = jnp.dot(activated_b.T, grad_b, preferred_element_type=jnp.float32)
    grad_activated = jnp.dot(grad_b, w_down.T, preferred_element_type=jnp.float32)
    grad_gate_up = swiglu_back(grad_activated)[0].astype(jnp.bfloat16)
    grad_w_gate_up = jnp.dot(normed_two_b.T, grad_gate_up, preferred_element_type=jnp.float32)
    grad_normed_two = jnp.dot(grad_gate_up, w_gate_up.T, preferred_element_type=jnp.float32)
    grad_resid_mlp, grad_gain_two = norm_two_back(grad_normed_two)
    grad_residual = grad_pack + grad_resid_mlp
    grad_mix_b = grad_residual.astype(jnp.bfloat16)
    grad_w_ssm_out = jnp.dot(gated_b.T, grad_mix_b, preferred_element_type=jnp.float32)
    grad_gated = jnp.dot(grad_mix_b, w_ssm_out.T, preferred_element_type=jnp.float32)
    grad_ssm_out, grad_ssm_gate = gate_back(grad_gated)
    grad_in, grad_write, grad_read, grad_step, grad_bias, grad_rate, grad_skip = ssm_back(grad_ssm_out)
    grad_extended, grad_conv_weight, grad_conv_bias = conv_back(jnp.concatenate([grad_in, grad_write, grad_read], axis=1))
    grad_projected = jnp.concatenate([grad_ssm_gate, grad_extended[KERNEL - 1:], grad_step], axis=1).astype(jnp.bfloat16)
    grad_w_attn_out = jnp.dot(attended_b.T, grad_mix_b, preferred_element_type=jnp.float32)
    grad_att_b = jnp.dot(grad_mix_b, w_attn_out.T, preferred_element_type=jnp.float32).astype(jnp.bfloat16)
    grad_queries, gradient_keys, gradient_values = attend_back(queries, key_tile_rows, value_tile_rows, attended_b, grad_att_b, log_total, allowed)
    grad_qkv = jnp.concatenate([apply_rotary(grad_queries, cosine_table, sine_table, True), apply_rotary(gradient_keys, cosine_table, sine_table, True), gradient_values], axis=1).astype(jnp.bfloat16)
    grad_w_qkv = jnp.dot(normed_b.T, grad_qkv, preferred_element_type=jnp.float32)
    grad_w_in = jnp.dot(normed_b.T, grad_projected, preferred_element_type=jnp.float32)
    grad_normed_one = jnp.dot(grad_projected, w_in.T, preferred_element_type=jnp.float32) + jnp.dot(grad_qkv, w_qkv.T, preferred_element_type=jnp.float32)
    grad_resid_norm, grad_gain_one = norm_one_back(grad_normed_one)
    grad_input = grad_residual + grad_resid_norm
    mixer_grads = (grad_w_in, grad_w_ssm_out, grad_w_qkv, grad_w_attn_out, grad_conv_weight, grad_conv_bias, grad_gain_one, grad_bias, grad_rate, grad_skip)
    feed_grads = (grad_w_gate_up, grad_w_down, grad_gain_two)
    return (block_out, grad_input, mixer_grads, feed_grads)

def adam_step(weights, grads, first_state, second_state):
    first_next = beta_one * first_state + (1.0 - beta_one) * grads
    second_next = beta_two * second_state + (1.0 - beta_two) * grads * grads
    first_hat = first_next / (1.0 - beta_one ** STEP)
    second_hat = second_next / (1.0 - beta_two ** STEP)
    weight_next = weights - learn_rate * (first_hat / (jnp.sqrt(second_hat) + adam_eps) + decay_weight * weights)
    return (weight_next, first_next, second_next)

def reference(hidden_in, positions, mixer_params, feed_params, mixer_first, feed_first, mixer_second, feed_second, out_grad):
    mixer = unflatten(mixer_params.astype(jnp.bfloat16).reshape(-1), mixer_layouts())
    feed = unflatten(feed_params.astype(jnp.bfloat16).reshape(-1), feed_layouts())
    pack_count = hidden_in.shape[0] // PACK
    inputs = (hidden_in.reshape(pack_count, PACK, D), positions.reshape(pack_count, PACK), out_grad.reshape(pack_count, PACK, D))
    start_grads = (tuple((jnp.zeros(member.shape, jnp.float32) for member in mixer)), tuple((jnp.zeros(member.shape, jnp.float32) for member in feed)))

    def visit(carry, packed):
        block_out, grad_input, mixer_grads, feed_grads = pack_pass(packed[0], packed[1], packed[2], mixer, feed)
        mixer_sum = tuple((left + right for left, right in zip(carry[0], mixer_grads)))
        feed_sum = tuple((left + right for left, right in zip(carry[1], feed_grads)))
        return ((mixer_sum, feed_sum), (block_out, grad_input))
    (mixer_sum, feed_sum), (outputs, grad_inputs) = lax.scan(visit, start_grads, inputs)
    mixer_grad = pack_rows(mixer_sum, DEVICES, SA)
    feed_grad = pack_rows(feed_sum, DEVICES, SB)
    mixer_new, mixer_first_new, mixer_second_new = adam_step(mixer_params, mixer_grad, mixer_first, mixer_second)
    feed_new, feed_first_new, feed_second_new = adam_step(feed_params, feed_grad, feed_first, feed_second)
    return (outputs.reshape(TOKENS, D), grad_inputs.reshape(TOKENS, D), mixer_grad, feed_grad, mixer_new, feed_new, mixer_first_new, feed_first_new, mixer_second_new, feed_second_new)
```

```python
import math

import jax
import jax.numpy as jnp
from jax import lax
from jax.sharding import PartitionSpec as P

D = 1024
FF = 2048
HEADS_SSM = 24
HEAD_SSM = 64
STATE = 128
KERNEL = 4
HEADS = 8
KV_HEADS = 2
HD = 64
STEP = 10
DI = 1536
CONV_COLS = 1792
QUERY_CHANNELS = 512
KEY_CHANNELS = 128
IN_COLS = 3352
QKV_COLS = 768
LANE = 128
WIDE = 1024
SMALL = KERNEL * CONV_COLS + CONV_COLS + D + 3 * HEADS_SSM

eps_norm = 1e-05
rope_base = 100000000000.0
neg_large = -1e30
beta_one = 0.9
beta_two = 0.95
learn_rate = 0.01
decay_weight = 0.1
adam_eps = 1e-08
highest = lax.Precision.HIGHEST
f32 = jnp.float32
bf16 = jnp.bfloat16


def swap(x, axis, bit):
    n = lax.axis_size(axis)
    return lax.ppermute(x, axis, [(i, i ^ bit) for i in range(n)])


def ctx_gather(x):
    n, place = lax.axis_size("ctx"), lax.axis_index("ctx")
    held, bit = x[None], n >> 1
    while bit:
        other = swap(held, "ctx", bit)
        upper = (place & bit) != 0
        low, high = jnp.where(upper, other, held), jnp.where(upper, held, other)
        held = jnp.stack([low, high], axis=1).reshape((-1,) + x.shape)
        bit >>= 1
    return held


def ctx_scatter(x):
    n, place = lax.axis_size("ctx"), lax.axis_index("ctx")
    held, bit = x, 1
    while bit < n:
        halves = held.reshape((held.shape[0] // 2, 2) + x.shape[1:])
        mine = jnp.where((place & bit) != 0, 1, 0)
        keep = lax.dynamic_index_in_dim(halves, mine, 1, False)
        send = lax.dynamic_index_in_dim(halves, 1 - mine, 1, False)
        held = keep + swap(send.astype(bf16), "ctx", bit).astype(f32)
        bit <<= 1
    return held[0]


def all_sum(x):
    for axis in ("ctx", "dp"):
        bit = 1
        while bit < lax.axis_size(axis):
            x = x + swap(x, axis, bit)
            bit <<= 1
    return x


def line_pairs(n, shift, last):
    length = n // 2
    result = []
    for z in range(length):
        to = z + shift
        far = z + last if shift > 0 else z - last
        if 0 <= to < length and 0 <= far < length:
            result += [(2 * z + y, 2 * to + y) for y in (0, 1)]
    return result


def pair_up(x, y, n, ok):
    pairs = [(i, i ^ 1) for i in range(n) if ok(i // 2)]
    other = lax.ppermute(x, "dp", pairs)
    upper = y != 0
    return jnp.stack([jnp.where(upper, other, x), jnp.where(upper, x, other)])


def dp_gather(x):
    n, place = lax.axis_size("dp"), lax.axis_index("dp")
    if n != 8:
        every = lax.all_gather(x, "dp")
        return lambda i, lo, hi: every[i, lo:hi]
    length = n // 2
    z, y = place // 2, place % 2
    right, left = x, x
    line = [pair_up(x, y, n, lambda z: True)]
    for k in range(1, length):
        right = lax.ppermute(right, "dp", [(i, i + 2) for i in range(n) if i // 2 >= k - 1 and i + 2 < n])
        left = lax.ppermute(left, "dp", [(i, i - 2) for i in range(n) if i // 2 <= length - k and i - 2 >= 0])
        line = (
            [pair_up(right, y, n, lambda z: z >= k)]
            + line
            + [pair_up(left, y, n, lambda z: z < length - k)]
        )
    line = jnp.stack(line)

    def get(i, lo, hi):
        at = length - 1 - z + i // 2
        return lax.dynamic_slice(
            line, (at, i % 2, lo, 0), (1, 1, hi - lo, x.shape[1])
        ).reshape(hi - lo, x.shape[1])

    return get


def dp_scatter(x):
    n, place = lax.axis_size("dp"), lax.axis_index("dp")
    if n != 8:
        flat = x.reshape((n * x.shape[1],) + x.shape[2:])
        return lax.psum_scatter(flat, "dp", scatter_dimension=0, tiled=True).astype(f32)
    length = n // 2
    z, y = place // 2, place % 2

    def joined(distance, ok):
        to = jnp.clip(z + distance, 0, length - 1)
        mine = lax.dynamic_index_in_dim(x, 2 * to + y, 0, False)
        theirs = lax.dynamic_index_in_dim(x, 2 * to + 1 - y, 0, False)
        pairs = [(i, i ^ 1) for i in range(n) if ok(i // 2)]
        return mine.astype(f32) + lax.ppermute(theirs, "dp", pairs).astype(f32)

    from_left = from_right = None
    for k in range(length - 1, 0, -1):
        right = joined(k, lambda z: z + k < length)
        left = joined(-k, lambda z: z - k >= 0)
        if from_left is not None:
            right, left = right + from_left, left + from_right
        from_left = lax.ppermute(
            right.astype(bf16), "dp", [(i, i + 2) for i in range(n) if i // 2 + k < length]
        ).astype(f32)
        from_right = lax.ppermute(
            left.astype(bf16), "dp", [(i, i - 2) for i in range(n) if i // 2 - k >= 0]
        ).astype(f32)
    return joined(0, lambda z: True) + from_left + from_right


def up(value, step):
    return -(-value // step) * step


class Piece:
    pass


def plan_group(mats, blocks, window, n):
    widest = LANE
    while widest < window // mats[0][2] + 32:
        widest *= 2
    plan, rows_max = [], 0
    for i in range(blocks):
        pieces, row, start = [], 0, 0
        for which, (kind, rows, width) in enumerate(mats):
            stop = start + rows * width
            lo, hi = max(start, i * window), min(stop, (i + 1) * window)
            if lo < hi:
                p = Piece()
                p.which, p.kind, p.width, p.lo, p.hi, p.start = which, kind, width, lo, hi, start
                first, last = (lo - start) // width, -(-(hi - start) // width)
                if kind == "rows":
                    p.r0, p.r1 = first // (LANE * n) * LANE * n, up(last, LANE * n)
                    spans = []
                    for c in range(n):
                        owned = [
                            r // (LANE * n) * LANE + r % LANE
                            for r in range(first, last)
                            if r // LANE % n == c
                        ]
                        if owned:
                            spans.append((owned[0], owned[-1] + 1))
                    p.t0 = min(s for s, _ in spans) // 16 * 16
                    p.t1 = up(max(e for _, e in spans), 16)
                    p.count = p.t1 - p.t0
                elif kind == "qkv":
                    p.r0, p.r1 = first // 64 * 64, up(last, 64)
                    p.count = (p.r1 - p.r0) // 4
                else:
                    p.r0, p.r1 = first // 16 * 16, up(last, 16)
                    p.count = p.r1 - p.r0
                p.row = row
                row += p.count
                if kind == "in":
                    p.lanes = widest
                    p.extra = row
                    row += up(HEADS_SSM * widest // WIDE, 16)
                pieces.append(p)
            start = stop
        plan.append(pieces)
        rows_max = max(rows_max, row)
    return plan, rows_max


def mixer_mats():
    return [
        ("in", D, IN_COLS),
        ("rows", DI, D),
        ("qkv", D, QKV_COLS),
        ("rows", QUERY_CHANNELS, D),
        ("same", up(SMALL, WIDE) // WIDE, WIDE),
    ]


def feed_mats():
    return [("up", D, 2 * FF), ("rows", FF, D), ("same", 1, D)]


def own_blocks(x, first, count, n, place):
    result = []
    for j in range(count // n):
        at = first + j * n * LANE
        block = x[:, at : at + LANE]
        for c in range(1, n):
            block = jnp.where(place == c, x[:, at + c * LANE : at + (c + 1) * LANE], block)
        result.append(block)
    return result


def all_blocks(x, first, count, n, place):
    result = []
    for b in range(count):
        block = x[:, first + b // n * LANE : first + (b // n + 1) * LANE]
        result.append(jnp.where(place == b % n, block, jnp.zeros_like(block)))
    return result


def pick_message(pieces, rows_max, window, index, n, flat, place):
    parts, filled = [], 0
    for p in pieces:
        cut = flat[p.lo - index * window : p.hi - index * window]
        front = p.lo - p.start - p.r0 * p.width
        back = (p.r1 - p.r0) * p.width - front - (p.hi - p.lo)
        x = jnp.pad(cut, (front, back)).reshape(p.r1 - p.r0, p.width)
        rows = x.shape[0]
        if p.kind == "in":
            blocks = own_blocks(x, 0, DI // LANE, n, place) + own_blocks(x, DI, DI // LANE, n, place)
            blocks.append(x[:, 2 * DI : DI + CONV_COLS])
            parts.append(jnp.concatenate(blocks, axis=1))
            groups = WIDE // p.lanes
            each = HEADS_SSM // groups
            steps = jnp.pad(x[:, DI + CONV_COLS :].T, ((0, 0), (0, p.lanes - rows)))
            steps = jnp.concatenate([steps[g * each : (g + 1) * each] for g in range(groups)], axis=1)
            parts.append(jnp.pad(steps, ((0, up(each, 16) - each), (0, 0))))
        elif p.kind == "up":
            blocks = own_blocks(x, 0, FF // LANE, n, place) + own_blocks(x, FF, FF // LANE, n, place)
            parts.append(jnp.concatenate(blocks, axis=1))
        elif p.kind == "rows":
            x = x.reshape(rows // (LANE * n), n, LANE, WIDE)
            x = lax.dynamic_index_in_dim(x, place, 1, False).reshape(rows // n, WIDE)
            base = p.r0 // n
            parts.append(x[p.t0 - base : p.t1 - base])
        elif p.kind == "qkv":
            per = QUERY_CHANNELS // n
            half = place * KV_HEADS // n
            q = x[:, :per]
            for c in range(1, n):
                q = jnp.where(place == c, x[:, c * per : (c + 1) * per], q)
            kv = []
            for first in (QUERY_CHANNELS, QUERY_CHANNELS + KEY_CHANNELS):
                kv.append(
                    jnp.where(half == 0, x[:, first : first + HD], x[:, first + HD : first + 2 * HD])
                )
            x = jnp.concatenate([q] + kv, axis=1)
            parts.append(
                jnp.concatenate([x[g * p.count : (g + 1) * p.count] for g in range(4)], axis=1)
            )
        else:
            parts.append(x)
        filled = p.row + p.count
        if p.kind == "in":
            filled = p.extra + up(HEADS_SSM * p.lanes // WIDE, 16)
    if filled < rows_max:
        parts.append(jnp.zeros((rows_max - filled, WIDE), flat.dtype))
    return jnp.concatenate(parts, axis=0)


def join_message(plan, which, rows, get):
    total = None
    for i, pieces in enumerate(plan):
        for p in pieces:
            if p.which != which:
                continue
            x = get(i, p.row, p.row + p.count)
            first = p.r0
            if p.kind == "rows":
                first = p.t0
            if p.kind == "qkv":
                x = jnp.concatenate([x[:, g * 256 : (g + 1) * 256] for g in range(4)], axis=0)
            x = x[: rows - first]
            x = jnp.pad(x, ((first, rows - first - x.shape[0]), (0, 0)))
            total = x if total is None else total + x
    return total


def join_steps(plan, get):
    total = None
    for i, pieces in enumerate(plan):
        for p in pieces:
            if p.kind != "in":
                continue
            groups = WIDE // p.lanes
            each = HEADS_SSM // groups
            x = get(i, p.extra, p.extra + up(each, 16))[:each]
            x = jnp.concatenate([x[:, g * p.lanes : (g + 1) * p.lanes] for g in range(groups)], axis=0)
            count = min(p.r1, D) - p.r0
            x = jnp.pad(x[:, :count], ((0, 0), (p.r0, D - p.r0 - count)))
            total = x if total is None else total + x
    return total


def fill_message(pieces, rows_max, grads, steps):
    parts, filled = [], 0

    def rows_of(x, lo, hi):
        have = x[lo : min(hi, x.shape[0])]
        return jnp.pad(have, ((0, hi - lo - have.shape[0]), (0, 0)))

    for p in pieces:
        x = grads[p.which]
        if p.kind == "rows":
            parts.append(rows_of(x, p.t0, p.t1))
        elif p.kind == "qkv":
            parts.append(
                jnp.concatenate(
                    [rows_of(x, p.r0 + g * p.count, p.r0 + (g + 1) * p.count) for g in range(4)], axis=1
                )
            )
        else:
            parts.append(rows_of(x, p.r0, p.r1))
        filled = p.row + p.count
        if p.kind == "in":
            groups = WIDE // p.lanes
            each = HEADS_SSM // groups
            count = min(p.r1, D) - p.r0
            part = jnp.pad(steps[:, p.r0 : p.r0 + count], ((0, 0), (0, p.lanes - count)))
            part = jnp.concatenate([part[g * each : (g + 1) * each] for g in range(groups)], axis=1)
            parts.append(jnp.pad(part, ((0, up(each, 16) - each), (0, 0))))
            filled = p.extra + up(each, 16)
    if filled < rows_max:
        parts.append(jnp.zeros((rows_max - filled, WIDE), bf16))
    return jnp.concatenate(parts, axis=0)


def spread_message(pieces, window, index, n, message, extra_one, place):
    parts, filled = [], 0
    for p in pieces:
        x = message[p.row : p.row + p.count]
        rows = p.r1 - p.r0
        if p.kind == "in":
            groups = WIDE // p.lanes
            each = HEADS_SSM // groups
            steps = message[p.extra : p.extra + each]
            steps = jnp.concatenate(
                [steps[:, g * p.lanes : (g + 1) * p.lanes] for g in range(groups)], axis=0
            )
            steps = steps[:, :rows].T
            own = DI // n
            blocks = all_blocks(x, 0, DI // LANE, n, place) + all_blocks(x, own, DI // LANE, n, place)
            x = jnp.concatenate(blocks + [x[:, 2 * own : 2 * own + 2 * STATE], steps], axis=1)
        elif p.kind == "up":
            own = FF // n
            blocks = all_blocks(x, 0, FF // LANE, n, place) + all_blocks(x, own, FF // LANE, n, place)
            x = jnp.concatenate(blocks, axis=1)
        elif p.kind == "rows":
            base = p.r0 // n
            x = jnp.pad(x, ((p.t0 - base, p.r1 // n - p.t1), (0, 0)))
            x = x.reshape(rows // (LANE * n), 1, LANE, WIDE)
            at = jnp.arange(n, dtype=jnp.int32)[None, :, None, None] == place
            x = jnp.where(at, x, jnp.zeros((), x.dtype)).reshape(rows, WIDE)
        elif p.kind == "qkv":
            x = jnp.concatenate([x[:, g * 256 : (g + 1) * 256] for g in range(4)], axis=0)
            per = QUERY_CHANNELS // n
            half = place * KV_HEADS // n
            zero = jnp.zeros((), x.dtype)
            blocks = [jnp.where(place == c, x[:, :per], zero) for c in range(n)]
            for first in (per, per + HD):
                blocks += [jnp.where(half == h, x[:, first : first + HD], zero) for h in range(KV_HEADS)]
            x = jnp.concatenate(blocks, axis=1)
        elif extra_one is not None:
            x = x[: extra_one.shape[0] + p.r0][: p.r1 - p.r0]
            more = extra_one[p.r0 : p.r1]
            more = jnp.pad(more, ((0, x.shape[0] - more.shape[0]), (0, 0)))
            x = x + jnp.where(place == 0, more, jnp.zeros((), x.dtype))
        front = p.lo - p.start - p.r0 * p.width
        parts.append(x.reshape(-1)[front : front + p.hi - p.lo])
        filled = p.hi - index * window
    if filled < window:
        parts.append(jnp.zeros((window - filled,), message.dtype))
    return jnp.concatenate(parts) if len(parts) > 1 else parts[0]


def distribute(shard, plan, rows_max, n):
    place, at = lax.axis_index("ctx"), lax.axis_index("dp")
    width = shard.shape[1]
    window = n * width
    flat = ctx_gather(shard.astype(bf16).reshape(width // LANE, LANE)).reshape(-1)
    branches = [
        (lambda flat, place, i=i: pick_message(plan[i], rows_max, window, i, n, flat, place))
        for i in range(len(plan))
    ]
    return dp_gather(lax.switch(at, branches, flat, place))


def collect(plan, rows_max, n, width, grads, steps, extra_one=None):
    place, at = lax.axis_index("ctx"), lax.axis_index("dp")
    window = n * width
    rows = jnp.stack([fill_message(pieces, rows_max, grads, steps) for pieces in plan])
    message = dp_scatter(rows)
    if extra_one is None:
        branches = [
            (lambda m, place, i=i: spread_message(plan[i], window, i, n, m, None, place))
            for i in range(len(plan))
        ]
        flat = lax.switch(at, branches, message, place)
    else:
        branches = [
            (lambda m, e, place, i=i: spread_message(plan[i], window, i, n, m, e, place))
            for i in range(len(plan))
        ]
        flat = lax.switch(at, branches, message, extra_one, place)
    return ctx_scatter(flat.reshape(n, width // LANE, LANE)).reshape(1, width)


def rms_scale(values):
    return lax.rsqrt(jnp.mean(values * values, axis=-1, keepdims=True) + eps_norm)


def rms_back(values, gain, grad):
    scale = rms_scale(values)
    unit = values * scale
    inner = grad * gain
    grad_values = scale * (inner - unit * jnp.mean(inner * unit, axis=-1, keepdims=True))
    return grad_values, jnp.sum(grad * unit, axis=0)


def swiglu(gate_up):
    half = gate_up.shape[1] // 2
    return jax.nn.silu(gate_up[:, :half]) * gate_up[:, half:]


def gate_product(ssm_out, ssm_gate):
    return ssm_out * jax.nn.silu(ssm_gate)


def causal_conv(positions, conv_input, conv_weight, conv_bias):
    row_count = positions.shape[0]
    extended = jnp.pad(conv_input, ((KERNEL - 1, 0), (0, 0)))
    summed = jnp.broadcast_to(conv_bias[None, :], conv_input.shape)
    for tap_index in range(KERNEL):
        first_row = KERNEL - 1 - tap_index
        earlier = extended[first_row : first_row + row_count]
        usable = (positions >= tap_index).astype(f32)[:, None]
        summed = summed + usable * earlier * conv_weight[tap_index][None, :]
    return jax.nn.silu(summed)


def rope_tables(positions):
    half_dim = HD // 2
    frequency = jnp.exp(-jnp.log(rope_base) * jnp.arange(half_dim, dtype=f32) * 2.0 / HD)
    angles = positions.astype(f32)[:, None] * frequency[None, :]
    return (jnp.cos(angles), jnp.sin(angles))


def apply_rotary(values, cosine_table, sine_table, reverse):
    row_count = values.shape[0]
    half_dim = HD // 2
    per_head = values.reshape(row_count, -1, HD)
    first_half = per_head[..., :half_dim]
    second_half = per_head[..., half_dim:]
    cos_wide = cosine_table[:, None, :]
    sin_wide = sine_table[:, None, :]
    if reverse:
        sin_wide = -sin_wide
    rotated = jnp.concatenate(
        [
            first_half * cos_wide - second_half * sin_wide,
            second_half * cos_wide + first_half * sin_wide,
        ],
        axis=-1,
    )
    return rotated.reshape(row_count, -1)


def attention_mask(positions):
    index = jnp.arange(positions.shape[0], dtype=jnp.int32)
    return (index[None, :] <= index[:, None]) & (index[None, :] >= (index - positions)[:, None])


def attend(queries, keys, values, allowed):
    row_count = queries.shape[0]
    heads = queries.reshape(row_count, -1, HD)
    scores = jnp.einsum("rhd,sd->hrs", heads, keys, preferred_element_type=f32) * HD ** (-0.5)
    unnormed = jnp.exp(jnp.where(allowed[None], scores, neg_large))
    row_sum = jnp.sum(unnormed, axis=-1, keepdims=True)
    mixed = (
        jnp.einsum("hrs,sd->hrd", unnormed.astype(bf16), values, preferred_element_type=f32) / row_sum
    )
    attended = jnp.transpose(mixed, (1, 0, 2)).reshape(row_count, -1)
    return attended, jnp.log(row_sum[..., 0])


def attend_back(queries, keys, values, attended_b, grad_att_b, log_total, allowed):
    row_count = queries.shape[0]
    heads = queries.reshape(row_count, -1, HD)
    scores = jnp.einsum("rhd,sd->hrs", heads, keys, preferred_element_type=f32) * HD ** (-0.5)
    probs = jnp.exp(jnp.where(allowed[None], scores - log_total[..., None], neg_large))
    gradient_heads = grad_att_b.reshape(row_count, -1, HD)
    out_heads = attended_b.reshape(row_count, -1, HD)
    grad_probs = jnp.einsum("rhd,sd->hrs", gradient_heads, values, preferred_element_type=f32)
    row_dot = jnp.sum(gradient_heads.astype(f32) * out_heads.astype(f32), axis=-1).T
    gradient_scores = (probs * (grad_probs - row_dot[..., None]) * HD ** (-0.5)).astype(bf16)
    grad_queries = jnp.einsum("hrs,sd->rhd", gradient_scores, keys, preferred_element_type=f32)
    gradient_keys = jnp.einsum("hrs,rhd->sd", gradient_scores, heads, preferred_element_type=f32)
    gradient_values = jnp.einsum(
        "hrs,rhd->sd", probs.astype(bf16), gradient_heads, preferred_element_type=f32
    )
    return grad_queries.reshape(row_count, -1), gradient_keys, gradient_values


def ssm(allowed, ssm_input, state_write, state_read, step_raw, bias_step, log_rate, skip_gain):
    row_count = ssm_input.shape[0]
    step_size = jax.nn.softplus(step_raw + bias_step[None, :])
    log_step = -jnp.exp(log_rate)[None, :] * step_size
    index = jnp.arange(row_count, dtype=jnp.int32)
    below = (index[None, :] <= index[:, None]).astype(f32)
    cumulative = jnp.dot(below, log_step, precision=highest)
    x = ssm_input.reshape(row_count, -1, HEAD_SSM)
    weighted = x * step_size[:, :, None]
    gaps = cumulative.T[:, :, None] - cumulative.T[:, None, :]
    decay = jnp.exp(jnp.where(allowed[None], gaps, neg_large))
    read_write = jnp.dot(state_read, state_write.T, precision=highest)
    out = jnp.einsum("hts,shp->thp", read_write[None] * decay, weighted, precision=highest)
    return (out + skip_gain[None, :, None] * x).reshape(row_count, -1)


def adam_step(weights, grads, first_state, second_state):
    first_next = beta_one * first_state + (1.0 - beta_one) * grads
    second_next = beta_two * second_state + (1.0 - beta_two) * grads * grads
    first_hat = first_next / (1.0 - beta_one**STEP)
    second_hat = second_next / (1.0 - beta_two**STEP)
    weight_next = weights - learn_rate * (
        first_hat / (jnp.sqrt(second_hat) + adam_eps) + decay_weight * weights
    )
    return (weight_next, first_next, second_next)


def dot(a, b):
    return jnp.dot(a, b, preferred_element_type=f32)


def dot_t(a, b):
    return lax.dot_general(a, b, (((1,), (1,)), ((), ())), preferred_element_type=f32)


def t_dot(a, b):
    return lax.dot_general(a, b, (((0,), (0,)), ((), ())), preferred_element_type=f32)


def body(
    hidden_in,
    positions,
    mixer_params,
    feed_params,
    mixer_first,
    feed_first,
    mixer_second,
    feed_second,
    out_grad,
):
    n, blocks = lax.axis_size("ctx"), lax.axis_size("dp")
    place = lax.axis_index("ctx")
    mixer_width, feed_width = mixer_params.shape[1], feed_params.shape[1]
    mixer_plan, mixer_rows = plan_group(mixer_mats(), blocks, n * mixer_width, n)
    feed_plan, feed_rows = plan_group(feed_mats(), blocks, n * feed_width, n)
    row_count = hidden_in.shape[0]

    get_mixer = distribute(mixer_params, mixer_plan, mixer_rows, n)
    positions = ctx_gather(positions[None])[:, 0].reshape(-1)
    out_grad_b = ctx_gather(out_grad.astype(bf16)).reshape(-1, D)

    own_di, own_q = DI // n, QUERY_CHANNELS // n
    w_in = join_message(mixer_plan, 0, D, get_mixer)
    w_ssm_out = join_message(mixer_plan, 1, DI // n, get_mixer)
    w_qkv = join_message(mixer_plan, 2, D, get_mixer)
    w_attn_out = join_message(mixer_plan, 3, own_q, get_mixer)
    small = join_message(mixer_plan, 4, up(SMALL, WIDE) // WIDE, get_mixer).reshape(-1).astype(f32)
    w_step = join_steps(mixer_plan, get_mixer)
    get_feed = distribute(feed_params, feed_plan, feed_rows, n)
    w_gate_up = join_message(feed_plan, 0, D, get_feed)
    w_down = join_message(feed_plan, 1, FF // n, get_feed)
    gain_two = join_message(feed_plan, 2, 1, get_feed).reshape(D).astype(f32)
    w_mix_out = jnp.concatenate([w_ssm_out, w_attn_out], axis=0)

    pairs = HEADS_SSM // (2 * n)

    def own_heads(x, axis):
        shape = x.shape[:axis] + (pairs, n, 2) + x.shape[axis + 1 :]
        picked = lax.dynamic_index_in_dim(x.reshape(shape), place, axis + 1, False)
        return picked.reshape(x.shape[:axis] + (2 * pairs,) + x.shape[axis + 1 :])

    def all_heads(x, axis):
        shape = x.shape[:axis] + (pairs, 1, 2) + x.shape[axis + 1 :]
        at = jnp.arange(n, dtype=jnp.int32) == place
        at = at.reshape((1,) * (axis + 1) + (n, 1) + (1,) * (x.ndim - axis - 1))
        spread = jnp.where(at, x.reshape(shape), jnp.zeros((), x.dtype))
        return spread.reshape(x.shape[:axis] + (HEADS_SSM,) + x.shape[axis + 1 :])

    def own_conv(x):
        parts = own_blocks(x, 0, DI // LANE, n, place)
        return jnp.concatenate(parts + [x[:, DI:]], axis=1)

    def all_conv(x):
        parts = all_blocks(x, 0, DI // LANE, n, place)
        return jnp.concatenate(parts + [x[:, own_di:]], axis=1)

    cut = KERNEL * CONV_COLS
    conv_weight = own_conv(small[:cut].reshape(KERNEL, CONV_COLS))
    conv_bias = own_conv(small[cut : cut + CONV_COLS].reshape(1, CONV_COLS))[0]
    cut += CONV_COLS
    gain_one = small[cut : cut + D]
    cut += D
    bias_step = own_heads(small[cut : cut + HEADS_SSM], 0)
    log_rate = own_heads(small[cut + HEADS_SSM : cut + 2 * HEADS_SSM], 0)
    skip_gain = own_heads(small[cut + 2 * HEADS_SSM : cut + 3 * HEADS_SSM], 0)
    w_step_own = own_heads(w_step, 0)

    normed_own = (hidden_in * rms_scale(hidden_in) * gain_one).astype(bf16)
    normed_b = ctx_gather(normed_own).reshape(-1, D)
    projected = dot(normed_b, w_in)
    step_raw = dot_t(normed_b, w_step_own)
    query_key_value = dot(normed_b, w_qkv)
    ssm_gate = projected[:, :own_di]
    conv_input = projected[:, own_di:]
    allowed = attention_mask(positions)
    conv_out, conv_back = jax.vjp(
        lambda a, w, b: causal_conv(positions, a, w, b), conv_input, conv_weight, conv_bias
    )
    ssm_out, ssm_back = jax.vjp(
        lambda *args: ssm(allowed, *args),
        conv_out[:, :own_di],
        conv_out[:, own_di : own_di + STATE],
        conv_out[:, own_di + STATE :],
        step_raw,
        bias_step,
        log_rate,
        skip_gain,
    )
    gated, gate_back = jax.vjp(gate_product, ssm_out, ssm_gate)
    cosine_table, sine_table = rope_tables(positions)
    queries = apply_rotary(query_key_value[:, :own_q], cosine_table, sine_table, False).astype(bf16)
    keys = apply_rotary(
        query_key_value[:, own_q : own_q + HD], cosine_table, sine_table, False
    ).astype(bf16)
    values = query_key_value[:, own_q + HD :].astype(bf16)
    attended, log_total = attend(queries, keys, values, allowed)
    mixed_b = jnp.concatenate([gated.astype(bf16), attended.astype(bf16)], axis=1)
    branches = ctx_scatter(dot(mixed_b, w_mix_out).reshape(n, row_count, D))
    residual = hidden_in + branches

    normed_two_own = (residual * rms_scale(residual) * gain_two).astype(bf16)
    normed_two_b = ctx_gather(normed_two_own).reshape(-1, D)
    gate_up = dot(normed_two_b, w_gate_up)
    activated, swiglu_back = jax.vjp(swiglu, gate_up)
    activated_b = activated.astype(bf16)
    block_out = residual + ctx_scatter(dot(activated_b, w_down).reshape(n, row_count, D))

    grad_w_down = t_dot(activated_b, out_grad_b).astype(bf16)
    grad_activated = dot_t(out_grad_b, w_down)
    grad_gate_up = swiglu_back(grad_activated)[0].astype(bf16)
    grad_normed_two = ctx_scatter(dot_t(grad_gate_up, w_gate_up).reshape(n, row_count, D))
    grad_w_gate_up = t_dot(normed_two_b, grad_gate_up).astype(bf16)
    grad_resid_mlp, grad_gain_two = rms_back(residual, gain_two, grad_normed_two)
    grad_residual = out_grad + grad_resid_mlp
    feed_grad = collect(
        feed_plan,
        feed_rows,
        n,
        feed_width,
        (grad_w_gate_up, grad_w_down, grad_gain_two.astype(bf16)[None]),
        None,
    )

    grad_mix_b = ctx_gather(grad_residual.astype(bf16)).reshape(-1, D)
    grad_mixed = dot_t(grad_mix_b, w_mix_out)
    grad_w_mix_out = t_dot(mixed_b, grad_mix_b).astype(bf16)
    grad_ssm_out, grad_ssm_gate = gate_back(grad_mixed[:, :own_di])
    grad_in, grad_write, grad_read, grad_step, grad_bias, grad_rate, grad_skip = ssm_back(grad_ssm_out)
    grad_conv_input, grad_conv_weight, grad_conv_bias = conv_back(
        jnp.concatenate([grad_in, grad_write, grad_read], axis=1)
    )
    grad_projected = jnp.concatenate([grad_ssm_gate, grad_conv_input], axis=1).astype(bf16)
    grad_step_b = grad_step.astype(bf16)
    grad_att_b = grad_mixed[:, own_di:].astype(bf16)
    grad_queries, grad_keys, grad_values = attend_back(
        queries, keys, values, mixed_b[:, own_di:], grad_att_b, log_total, allowed
    )
    grad_qkv = jnp.concatenate(
        [
            apply_rotary(grad_queries, cosine_table, sine_table, True),
            apply_rotary(grad_keys, cosine_table, sine_table, True),
            grad_values,
        ],
        axis=1,
    ).astype(bf16)
    partial_one = (
        dot_t(grad_projected, w_in) + dot_t(grad_qkv, w_qkv) + dot(grad_step_b, w_step_own)
    )
    grad_normed_one = ctx_scatter(partial_one.reshape(n, row_count, D))
    grad_w_in = t_dot(normed_b, grad_projected).astype(bf16)
    grad_w_qkv = t_dot(normed_b, grad_qkv).astype(bf16)
    grad_w_step = all_heads(t_dot(grad_step_b, normed_b).astype(bf16), 0)
    grad_resid_norm, grad_gain_one = rms_back(hidden_in, gain_one, grad_normed_one)
    grad_input = grad_residual + grad_resid_norm
    gain_sum = all_sum(grad_gain_one.reshape(D // LANE, LANE)).reshape(-1)
    before, after = KERNEL * CONV_COLS + CONV_COLS, 3 * HEADS_SSM
    small_size = up(SMALL, WIDE)
    gain_rows = jnp.pad(gain_sum, (before, small_size - before - D)).reshape(-1, WIDE)
    small_grads = jnp.concatenate(
        [
            all_conv(grad_conv_weight).reshape(-1),
            all_conv(grad_conv_bias[None])[0],
            jnp.zeros((D,), f32),
            all_heads(grad_bias, 0),
            all_heads(grad_rate, 0),
            all_heads(grad_skip, 0),
            jnp.zeros((small_size - SMALL,), f32),
        ]
    ).reshape(-1, WIDE)
    mixer_grad = collect(
        mixer_plan,
        mixer_rows,
        n,
        mixer_width,
        (
            grad_w_in,
            grad_w_mix_out[:own_di],
            grad_w_qkv,
            grad_w_mix_out[own_di:],
            small_grads.astype(bf16),
        ),
        grad_w_step,
        gain_rows,
    )

    mixer_new, mixer_first_new, mixer_second_new = adam_step(
        mixer_params, mixer_grad, mixer_first, mixer_second
    )
    feed_new, feed_first_new, feed_second_new = adam_step(
        feed_params, feed_grad, feed_first, feed_second
    )
    return (
        block_out,
        grad_input,
        mixer_grad,
        feed_grad,
        mixer_new,
        feed_new,
        mixer_first_new,
        feed_first_new,
        mixer_second_new,
        feed_second_new,
    )


def solution(mesh):
    in_specs = (
        P(("dp", "ctx"), None),
        P(("dp", "ctx")),
        P(("dp", "ctx"), None),
        P(("dp", "ctx"), None),
        P(("dp", "ctx"), None),
        P(("dp", "ctx"), None),
        P(("dp", "ctx"), None),
        P(("dp", "ctx"), None),
        P(("dp", "ctx"), None),
    )
    out_specs = (
        P(("dp", "ctx"), None),
        P(("dp", "ctx"), None),
        P(("dp", "ctx"), None),
        P(("dp", "ctx"), None),
        P(("dp", "ctx"), None),
        P(("dp", "ctx"), None),
        P(("dp", "ctx"), None),
        P(("dp", "ctx"), None),
        P(("dp", "ctx"), None),
        P(("dp", "ctx"), None),
    )
    return jax.shard_map(body, mesh=mesh, in_specs=in_specs, out_specs=out_specs, check_vma=False)
```
